32 devices in a mesh: lat: 8 (over y, x, core), lev: 4 (over z).
Axes of the slice: x: 2, y: 2, z: 4, core: 2. Of those that a mesh axis runs over, the one named last changes fastest.
Arguments:
- activations: bfloat16 [176, 819200], P(None, ('lat', 'lev')), may hold values from -6 to 6
- out_cotangent: bfloat16 [176, 819200], P(None, ('lat', 'lev')), may hold values from -6 to 6
- weight_in: bfloat16 [176, 384], replicated, may hold values from -0.4375 to 0.4375
- weight_mid: bfloat16 [384, 384], replicated, may hold values from -0.3125 to 0.3125
- weight_out: bfloat16 [176, 384], replicated, may hold values from -0.3125 to 0.3125
- legendre: bfloat16 [640, 320, 640], P(('lat', 'lev')), may hold values from -0.25 to 0.25
- level_inverse: bfloat16 [88, 88, 640], replicated, may hold values from -0.625 to 0.625
- wave_order: int32 [640], replicated, may hold values from 0 to 639, each once
Outputs:
- grad_input: float32 [176, 384], replicated
- grad_middle: float32 [384, 384], replicated
- grad_output: float32 [176, 384], replicated
- grid_cotangent: float32 [176, 640, 1280], P(None, ('lat', 'lev'))
The draws below stay inside these ranges and needn't reach their ends.
Inputs may be any that keep to these rules, and one draw needn't show every extreme that they name: wave_order is a permutation of 0 to 639; the device at index d of lat and lev taken together (lat major) holds the d-th block of slots of legendre.
All inputs are finite; a program needn't handle non-finite values.
Results may differ from the reference program's by a relative error of at most 0.017.
Values may be sent and summed in bfloat16 or wider, within the bound.
A program may use at most 320 MiB of HBM per device.

```python
import math
from functools import partial
import jax
import jax.numpy as jnp
from jax import lax

NLAT = 640
NLON = 1280
L = 88
H = 384
M = 640
F = 176
NDEG = 640
LATB = 80
LONB = 320
COLS = 819200
N_LAT = 8
N_LEV = 4


def steps_of(key, dims, shards, least, top_value):
    def one(position, blocks):
        draws = jax.random.uniform(jax.random.fold_in(jax.random.fold_in(key, 6), position), (blocks,), jnp.float32, least / len(shards), top_value / len(shards))
        return jnp.repeat(jnp.exp(draws), dims[position] // blocks).reshape((-1,) + (1,) * (len(dims) - position - 1))

    level = one(*shards[0])
    for cut in shards[1:]:
        level = level * one(*cut)
    return level


def bell_draw(key, extent, deviation, most, shards=(), kind=jnp.bfloat16):
    values = deviation * jax.random.normal(key, extent, jnp.float32)
    if shards:
        values = values * steps_of(key, extent, shards, -0.22, 0.18)
    return jnp.clip(values, -most, most).astype(kind)


def setup_inputs(seed: int = 0) -> dict:
    splits = jax.random.split(jax.random.key(seed), 9)
    return {
        "activations": bell_draw(splits[0], (F, COLS), 1.0, 6.0, ((1, 32),)),
        "out_cotangent": bell_draw(splits[1], (F, COLS), 1.0, 6.0, ((1, 32),)),
        "weight_in": bell_draw(splits[2], (F, H), F ** -0.5, 0.4375),
        "weight_mid": bell_draw(splits[3], (H, H), H ** -0.5, 0.3125),
        "weight_out": bell_draw(splits[4], (F, H), H ** -0.5, 0.3125),
        "legendre": bell_draw(splits[5], (M, NLAT // 2, NDEG), NLAT ** -0.5, 0.25, ((0, 32),)),
        "level_inverse": bell_draw(splits[6], (L, L, NDEG), L ** -0.5, 0.625),
        "wave_order": jax.random.permutation(splits[7], M).astype(jnp.int32),
    }


def silu_slope(values):
    sigmoid = jax.nn.sigmoid(values)
    return sigmoid * (1.0 + values * (1.0 - sigmoid))

def column_block(blocks, weight_in, weight_mid, weight_out):
    inputs, cotangents = blocks
    pre_first = jnp.dot(weight_in.T, inputs, preferred_element_type=jnp.float32)
    hidden_first = jax.nn.silu(pre_first).astype(jnp.bfloat16)
    pre_second = jnp.dot(weight_mid.T, hidden_first, preferred_element_type=jnp.float32)
    hidden_second = jax.nn.silu(pre_second).astype(jnp.bfloat16)
    back_second = jnp.dot(weight_out.T, cotangents, preferred_element_type=jnp.float32)
    delta_second = (back_second * silu_slope(pre_second)).astype(jnp.bfloat16)
    back_first = jnp.dot(weight_mid, delta_second, preferred_element_type=jnp.float32)
    delta_first = (back_first * silu_slope(pre_first)).astype(jnp.bfloat16)
    grid_part = jnp.dot(weight_in, delta_first, preferred_element_type=jnp.float32).astype(jnp.bfloat16)
    grad_first = jnp.dot(inputs, delta_first.T, preferred_element_type=jnp.float32)
    grad_second = jnp.dot(hidden_first, delta_second.T, preferred_element_type=jnp.float32)
    grad_third = jnp.dot(cotangents, hidden_second.T, preferred_element_type=jnp.float32)
    return (grid_part, grad_first, grad_second, grad_third)

def spectral_block(pieces, level_inverse):
    fourier, legendre_part, wave_local = pieces
    half_lat = NLAT // 2
    widened = fourier.astype(jnp.float32)
    north_rows = widened[..., :half_lat]
    south_rows = widened[..., half_lat:][..., ::-1]
    paired = jnp.stack([north_rows + south_rows, north_rows - south_rows]).astype(jnp.bfloat16)
    table_wide = legendre_part.astype(jnp.float32)
    result = jnp.einsum('ersfj,sjl->serfl', paired.astype(jnp.float32), table_wide)
    degree = jnp.arange(NDEG, dtype=jnp.int32)
    even_mask = (degree[None, :] + wave_local[:, None]) % 2 == 0
    keep_mask = degree[None, :] >= wave_local[:, None]
    even_wide = even_mask[:, None, None, :]
    coeffs = jnp.where(even_wide, result[:, 0], result[:, 1])
    coeffs = jnp.where(keep_mask[:, None, None, :], coeffs, 0.0).astype(jnp.bfloat16)
    slot_total = coeffs.shape[0]
    stacked = coeffs.reshape(slot_total, 2, 2, L, NDEG).astype(jnp.float32)
    solved = jnp.einsum('srakl,kil->srail', stacked, level_inverse.astype(jnp.float32))
    solved = solved.reshape(slot_total, 2, F, NDEG).astype(jnp.bfloat16)
    blank = jnp.zeros_like(solved)
    masked_parts = jnp.stack([jnp.where(even_wide, solved, blank), jnp.where(even_wide, blank, solved)])
    synthesized = jnp.einsum('esrfl,sjl->ersfj', masked_parts.astype(jnp.float32), table_wide)
    north_out = synthesized[0] + synthesized[1]
    south_out = synthesized[0] - synthesized[1]
    return jnp.concatenate([north_out, south_out[..., ::-1]], axis=-1).astype(jnp.bfloat16)

def reference(activations, out_cotangent, weight_in, weight_mid, weight_out, legendre, level_inverse, wave_order):
    block_cols = COLS // N_LAT
    blocks_in = activations.reshape(F, N_LAT, block_cols).transpose(1, 0, 2)
    blocks_cotangent = out_cotangent.reshape(F, N_LAT, block_cols).transpose(1, 0, 2)
    mapped = lax.map(partial(column_block, weight_in=weight_in, weight_mid=weight_mid, weight_out=weight_out), (blocks_in, blocks_cotangent))
    flat_grid = mapped[0].transpose(1, 0, 2).reshape(F, N_LAT, N_LEV, LATB, LONB)
    grid_input = flat_grid.transpose(0, 1, 3, 2, 4).reshape(F, NLAT, NLON)
    grad_scale = 1.0 / math.sqrt(NLAT * NLON)
    grad_input = lax.optimization_barrier(jnp.sum(mapped[1], axis=0)) * grad_scale
    grad_middle = lax.optimization_barrier(jnp.sum(mapped[2], axis=0)) * grad_scale
    grad_output = lax.optimization_barrier(jnp.sum(mapped[3], axis=0)) * grad_scale
    spectrum = jnp.fft.rfft(grid_input.astype(jnp.float32), axis=2) / math.sqrt(NLON)
    picked = jnp.take(spectrum, wave_order, axis=2)
    fourier = jnp.stack([picked.real, picked.imag]).transpose(0, 3, 1, 2).astype(jnp.bfloat16)
    group_size = M // N_LAT
    grouped = fourier.reshape(2, N_LAT, group_size, F, NLAT).transpose(1, 0, 2, 3, 4)
    tables = legendre.reshape(N_LAT, group_size, NLAT // 2, NDEG)
    wave_groups = wave_order.reshape(N_LAT, group_size)
    zonal_rows = lax.map(partial(spectral_block, level_inverse=level_inverse), (grouped, tables, wave_groups))
    zonal_rows = zonal_rows.transpose(1, 0, 2, 3, 4).reshape(2, M, F, NLAT).astype(jnp.float32)
    complex_rows = zonal_rows[0] + 1j * zonal_rows[1]
    full_spectrum = jnp.zeros((NLON // 2 + 1, F, NLAT), complex_rows.dtype).at[wave_order].set(complex_rows)
    grid_cotangent = (jnp.fft.irfft(full_spectrum, n=NLON, axis=0) * math.sqrt(NLON)).transpose(1, 2, 0)
    return (grad_input, grad_middle, grad_output, grid_cotangent)
```

```python
import math

import jax
import jax.numpy as jnp
from jax import lax
from jax.sharding import PartitionSpec as P

BF = jnp.bfloat16
F32 = jnp.float32


def silu_slope(values):
    sigmoid = jax.nn.sigmoid(values)
    return sigmoid * (1.0 + values * (1.0 - sigmoid))


def first_dims(left, right):
    return lax.dot_general(left, right, (((0,), (0,)), ((), ())), preferred_element_type=F32)


def last_dims(left, right):
    return lax.dot_general(left, right, (((1,), (1,)), ((), ())), preferred_element_type=F32)


def wave_tables(wavenumbers, points):
    wave_count = wavenumbers.shape[0]
    columns = lax.broadcasted_iota(jnp.int32, (points, wave_count), 0)
    phase_int = columns * wavenumbers[None, :] % points
    angles = phase_int.astype(F32) * (2.0 * math.pi / points)
    return (jnp.cos(angles), jnp.sin(angles))


def full_legendre(legendre, wave_local):
    slots, half, degrees = legendre.shape
    row = lax.broadcasted_iota(jnp.int32, (2 * half, half), 0)
    col = lax.broadcasted_iota(jnp.int32, (2 * half, half), 1)
    spread = ((row == col) | (row + col == 2 * half - 1)).astype(BF)
    both = jnp.einsum("pi,sil->spl", spread, legendre, preferred_element_type=F32)
    shape = (slots, 2 * half, degrees)
    degree = lax.broadcasted_iota(jnp.int32, shape, 2)
    lat = lax.broadcasted_iota(jnp.int32, shape, 1)
    wave = wave_local[:, None, None]
    flip = (lat >= half) & ((degree + wave) % 2 == 1)
    both = jnp.where(flip, -both, both)
    return jnp.where(degree >= wave, both, 0.0).astype(BF)


def on_device(
    activations,
    out_cotangent,
    weight_in,
    weight_mid,
    weight_out,
    legendre,
    level_inverse,
    wave_order,
):
    features, columns = activations.shape
    n_lat, n_lev = lax.axis_size("lat"), lax.axis_size("lev")
    n_dev = n_lat * n_lev
    slot_count, half, degrees = legendre.shape
    nlat = 2 * half
    levels = level_inverse.shape[0]
    fields = features // levels
    lat_rows = nlat // n_lat
    lon_rows = columns // lat_rows
    nlon = lon_rows * n_lev
    waves = wave_order.shape[0]
    sub = lat_rows // n_lev
    both_axes = ("lat", "lev")

    pre_first = first_dims(weight_in, activations)
    hidden_first = jax.nn.silu(pre_first).astype(BF)
    pre_second = first_dims(weight_mid, hidden_first)
    hidden_second = jax.nn.silu(pre_second).astype(BF)
    back_second = first_dims(weight_out, out_cotangent)
    delta_second = (back_second * silu_slope(pre_second)).astype(BF)
    back_first = jnp.dot(weight_mid, delta_second, preferred_element_type=F32)
    delta_first = (back_first * silu_slope(pre_first)).astype(BF)

    cosines, sines = wave_tables(wave_order, nlon)
    root_points = math.sqrt(nlon)
    forward_table = (jnp.stack([cosines, -sines], axis=2) / root_points).astype(BF)
    forward_table = forward_table.reshape(nlon, 2 * waves)
    wave_local = lax.dynamic_slice_in_dim(
        wave_order, lax.axis_index(both_axes) * slot_count, slot_count
    )
    table = full_legendre(legendre, wave_local)
    inverse_levels = level_inverse.transpose(2, 0, 1)
    wave_weights = jnp.where(wave_order > 0, 2.0, 1.0).astype(F32) / root_points
    inverse_table = (
        jnp.stack([cosines.T, -sines.T], axis=1) * wave_weights[:, None, None]
    ).astype(BF).reshape(2 * waves, nlon)

    grid_rows = []
    for a in range(fields):
        part = jnp.dot(
            weight_in[a * levels : (a + 1) * levels], delta_first, preferred_element_type=F32
        ).astype(BF)
        part = part.reshape(levels, n_lev, sub * lon_rows).transpose(1, 0, 2)
        grid_rows.append(lax.all_to_all(part, "lev", split_axis=0, concat_axis=0, tiled=True))

    partials = (
        last_dims(activations, delta_first),
        last_dims(hidden_first, delta_second),
        last_dims(out_cotangent, hidden_second),
    )
    forward_table, partials, grid_rows[0] = lax.optimization_barrier(
        (forward_table, partials, grid_rows[0])
    )
    totals = lax.psum(partials, both_axes)
    grad_scale = 1.0 / math.sqrt(nlat * nlon)

    gathered = []
    for a in range(fields):
        if a == fields - 1:
            table, inverse_levels, inverse_table, grid_rows[a] = lax.optimization_barrier(
                (table, inverse_levels, inverse_table, grid_rows[a])
            )
        rows = grid_rows[a].reshape(n_lev, levels, sub, lon_rows)
        rows = rows.transpose(2, 1, 0, 3).reshape(sub * levels, nlon)
        fourier = lax.dot_general(
            forward_table, rows, (((0,), (1,)), ((), ())), preferred_element_type=F32
        ).astype(BF)
        fourier = fourier.reshape(waves, 2, sub * levels)
        gathered.append(
            lax.all_to_all(fourier, both_axes, split_axis=0, concat_axis=0, tiled=True)
        )

    zonal = []
    for a in range(fields):
        fourier = gathered[a].reshape(n_dev, slot_count, 2, sub, levels)
        fourier = fourier.transpose(1, 2, 4, 0, 3).reshape(slot_count, 2 * levels, nlat)
        coeffs = jnp.einsum("sfi,sil->sfl", fourier, table, preferred_element_type=F32).astype(BF)
        coeffs = coeffs.reshape(slot_count, 2, levels, degrees)
        solved = jnp.einsum(
            "srkl,lkq->srql", coeffs, inverse_levels, preferred_element_type=F32
        ).astype(BF)
        rows = jnp.einsum("srql,sil->siqr", solved, table, preferred_element_type=F32).astype(BF)
        rows = rows.reshape(slot_count, n_dev, sub, levels, 2).transpose(1, 0, 4, 2, 3)
        rows = rows.reshape(waves, 2, sub * levels)
        zonal.append(lax.all_to_all(rows, both_axes, split_axis=0, concat_axis=0, tiled=True))

    outs = []
    for a in range(fields):
        out = lax.dot_general(
            zonal[a].reshape(2 * waves, sub * levels),
            inverse_table,
            (((0,), (0,)), ((), ())),
            preferred_element_type=F32,
        )
        outs.append(out.reshape(sub, levels, nlon))
    grid_cotangent = jnp.concatenate(outs, axis=1).transpose(1, 0, 2)
    return (totals[0] * grad_scale, totals[1] * grad_scale, totals[2] * grad_scale, grid_cotangent)


def solution(mesh):
    in_specs = (
        P(None, ("lat", "lev")),
        P(None, ("lat", "lev")),
        P(),
        P(),
        P(),
        P(("lat", "lev"), None, None),
        P(),
        P(),
    )
    out_specs = (P(), P(), P(), P(None, ("lat", "lev"), None))
    return jax.shard_map(
        on_device, mesh=mesh, in_specs=in_specs, out_specs=out_specs, check_vma=False
    )
```

```python
import math

import jax
import jax.numpy as jnp
from jax import lax
from jax.sharding import PartitionSpec as P

BF = jnp.bfloat16
F32 = jnp.float32


def silu_slope(values):
    sigmoid = jax.nn.sigmoid(values)
    return sigmoid * (1.0 + values * (1.0 - sigmoid))


def first_dims(left, right):
    return lax.dot_general(left, right, (((0,), (0,)), ((), ())), preferred_element_type=F32)


def last_dims(left, right):
    return lax.dot_general(left, right, (((1,), (1,)), ((), ())), preferred_element_type=F32)


def wave_tables(wavenumbers, points):
    wave_count = wavenumbers.shape[0]
    columns = lax.broadcasted_iota(jnp.int32, (points, wave_count), 0)
    phase_int = columns * wavenumbers[None, :] % points
    angles = phase_int.astype(F32) * (2.0 * math.pi / points)
    return (jnp.cos(angles), jnp.sin(angles))


def full_legendre(legendre, wave_local):
    slots, half, degrees = legendre.shape
    row = lax.broadcasted_iota(jnp.int32, (2 * half, half), 0)
    col = lax.broadcasted_iota(jnp.int32, (2 * half, half), 1)
    spread = ((row == col) | (row + col == 2 * half - 1)).astype(BF)
    both = jnp.einsum("pi,sil->spl", spread, legendre, preferred_element_type=F32)
    shape = (slots, 2 * half, degrees)
    degree = lax.broadcasted_iota(jnp.int32, shape, 2)
    lat = lax.broadcasted_iota(jnp.int32, shape, 1)
    wave = wave_local[:, None, None]
    flip = (lat >= half) & ((degree + wave) % 2 == 1)
    both = jnp.where(flip, -both, both)
    return jnp.where(degree >= wave, both, 0.0).astype(BF)


def on_device(
    activations,
    out_cotangent,
    weight_in,
    weight_mid,
    weight_out,
    legendre,
    level_inverse,
    wave_order,
):
    features, columns = activations.shape
    n_lat, n_lev = lax.axis_size("lat"), lax.axis_size("lev")
    n_dev = n_lat * n_lev
    slot_count, half, degrees = legendre.shape
    nlat = 2 * half
    levels = level_inverse.shape[0]
    fields = features // levels
    lat_rows = nlat // n_lat
    lon_rows = columns // lat_rows
    nlon = lon_rows * n_lev
    waves = wave_order.shape[0]
    sub = lat_rows // n_lev
    both_axes = ("lat", "lev")

    pre_first = first_dims(weight_in, activations)
    hidden_first = jax.nn.silu(pre_first).astype(BF)
    pre_second = first_dims(weight_mid, hidden_first)
    hidden_second = jax.nn.silu(pre_second).astype(BF)
    back_second = first_dims(weight_out, out_cotangent)
    delta_second = (back_second * silu_slope(pre_second)).astype(BF)
    back_first = jnp.dot(weight_mid, delta_second, preferred_element_type=F32)
    delta_first = (back_first * silu_slope(pre_first)).astype(BF)

    cosines, sines = wave_tables(wave_order, nlon)
    root_points = math.sqrt(nlon)
    forward_table = (jnp.stack([cosines, -sines], axis=2) / root_points).astype(BF)
    forward_table = forward_table.reshape(nlon, 2 * waves)
    wave_local = lax.dynamic_slice_in_dim(
        wave_order, lax.axis_index(both_axes) * slot_count, slot_count
    )
    table = full_legendre(legendre, wave_local)
    inverse_levels = level_inverse.transpose(2, 0, 1)
    wave_weights = jnp.where(wave_order > 0, 2.0, 1.0).astype(F32) / root_points
    inverse_table = (
        jnp.stack([cosines.T, -sines.T], axis=1) * wave_weights[:, None, None]
    ).astype(BF).reshape(2 * waves, nlon)

    grid_rows = []
    for a in range(fields):
        part = jnp.dot(
            weight_in[a * levels : (a + 1) * levels], delta_first, preferred_element_type=F32
        ).astype(BF)
        part = part.reshape(levels, n_lev, sub * lon_rows).transpose(1, 0, 2)
        grid_rows.append(lax.all_to_all(part, "lev", split_axis=0, concat_axis=0, tiled=True))

    partials = (
        last_dims(activations, delta_first),
        last_dims(hidden_first, delta_second),
        last_dims(out_cotangent, hidden_second),
    )
    forward_table, partials, grid_rows[0] = lax.optimization_barrier(
        (forward_table, partials, grid_rows[0])
    )
    totals = lax.psum(partials, both_axes)
    grad_scale = 1.0 / math.sqrt(nlat * nlon)

    gathered = []
    for a in range(fields):
        if a == fields - 1:
            table, inverse_levels, inverse_table, grid_rows[a] = lax.optimization_barrier(
                (table, inverse_levels, inverse_table, grid_rows[a])
            )
        rows = grid_rows[a].reshape(n_lev, levels, sub, lon_rows)
        rows = rows.transpose(2, 1, 0, 3).reshape(sub * levels, nlon)
        fourier = lax.dot_general(
            forward_table, rows, (((0,), (1,)), ((), ())), preferred_element_type=F32
        ).astype(BF)
        fourier = fourier.reshape(waves, 2, sub * levels)
        gathered.append(
            lax.all_to_all(fourier, both_axes, split_axis=0, concat_axis=0, tiled=True)
        )

    zonal = []
    for a in range(fields):
        if a == fields - 1:
            totals, gathered[a] = lax.optimization_barrier((totals, gathered[a]))
        fourier = gathered[a].reshape(n_dev, slot_count, 2, sub, levels)
        fourier = fourier.transpose(1, 2, 4, 0, 3).reshape(slot_count, 2 * levels, nlat)
        coeffs = jnp.einsum("sfi,sil->sfl", fourier, table, preferred_element_type=F32).astype(BF)
        coeffs = coeffs.reshape(slot_count, 2, levels, degrees)
        solved = jnp.einsum(
            "srkl,lkq->srql", coeffs, inverse_levels, preferred_element_type=F32
        ).astype(BF)
        rows = jnp.einsum("srql,sil->siqr", solved, table, preferred_element_type=F32).astype(BF)
        rows = rows.reshape(slot_count, n_dev, sub, levels, 2).transpose(1, 0, 4, 2, 3)
        rows = rows.reshape(waves, 2, sub * levels)
        zonal.append(lax.all_to_all(rows, both_axes, split_axis=0, concat_axis=0, tiled=True))

    outs = []
    for a in range(fields):
        out = lax.dot_general(
            zonal[a].reshape(2 * waves, sub * levels),
            inverse_table,
            (((0,), (0,)), ((), ())),
            preferred_element_type=F32,
        )
        outs.append(out.reshape(sub, levels, nlon))
    grid_cotangent = jnp.concatenate(outs, axis=1).transpose(1, 0, 2)
    return (totals[0] * grad_scale, totals[1] * grad_scale, totals[2] * grad_scale, grid_cotangent)


def solution(mesh):
    in_specs = (
        P(None, ("lat", "lev")),
        P(None, ("lat", "lev")),
        P(),
        P(),
        P(),
        P(("lat", "lev"), None, None),
        P(),
        P(),
    )
    out_specs = (P(), P(), P(), P(None, ("lat", "lev"), None))
    return jax.shard_map(
        on_device, mesh=mesh, in_specs=in_specs, out_specs=out_specs, check_vma=False
    )
```
